32 devices in a mesh: grid: 1, orb: 32 (over z, y, x, core).
Axes of the slice: x: 2, y: 2, z: 4, core: 2. Of those that a mesh axis runs over, the one named last changes fastest.
Arguments:
- orbitals: bfloat16 [512, 64, 4096], P('orb', 'grid'), may hold values from -6 to 6
- pairs: int32 [128, 4], P('orb'), may hold values from -16 to 511, as said below
- tiles: int32 [32, 2], replicated, may hold values from 0 to 31, as said below
Outputs:
- exch_force: float32 [512, 64, 4096], P('orb', 'grid')
- intersection_tiles: float32 [32, 256], P(('grid', 'orb'))
- self_intersection: float32 [512], P('orb')
The draws below stay inside these ranges and needn't reach their ends.
Inputs may be any that keep to these rules, and one draw needn't show every extreme that they name: In the pairs of one device (aligned blocks of 4 rows) at most 2 of the orbital entries (columns i and j) belong to one owner (an owner holds 16 consecutive orbitals), and those entries name at most 2 distinct orbitals of that owner, so an orbital may recur; both bounds are reached in every block. Offsets lie in -16 to 16. `tiles`: A listed tile's column block differs from its row block.
All inputs are finite; a program needn't handle non-finite values.
Results may differ from the reference program's by a relative error of at most 0.0058.
Values may be sent and summed in bfloat16 or wider, within the bound.
A program may use at most 256 MiB of HBM per device.

```python
import jax
import jax.numpy as jnp
from jax import lax

BOX = 64
ORB_DEV = 16
PAIR_DEV = 4
SWEEPS = 3
NORB = 512
NPAIRS = 128
NTILES = 32
REF_CAP = 2
SHIFT = 16
N_ORB = 32


def pair_block(block_key):
    keys = jax.random.split(block_key, 7)
    ref_count = 2 * PAIR_DEV
    first_owner = jax.random.randint(keys[0], (), 0, N_ORB)
    owner_slots = jnp.repeat(jnp.arange(N_ORB, dtype=jnp.int32), REF_CAP)
    owner_slots = jax.random.permutation(keys[1], owner_slots)
    ordering = jnp.argsort((owner_slots == first_owner).astype(jnp.int32), stable=True)
    others = owner_slots[ordering][:ref_count - REF_CAP]
    owners = jnp.concatenate([jnp.full((REF_CAP,), first_owner, jnp.int32), others])
    choice_a = jax.random.randint(keys[2], (N_ORB,), 0, ORB_DEV)
    stride_b = jax.random.randint(keys[3], (N_ORB,), 1, ORB_DEV)
    choice_b = (choice_a + stride_b) % ORB_DEV
    picker = jax.random.randint(keys[4], (ref_count,), 0, 2)
    picker = picker.at[0].set(0).at[1].set(1)
    local_index = jnp.where(picker == 0, choice_a[owners], choice_b[owners])
    orbital_ids = jax.random.permutation(keys[5], owners * ORB_DEV + local_index)
    offsets = jax.random.randint(keys[6], (PAIR_DEV, 2), -SHIFT, SHIFT + 1)
    return jnp.concatenate([orbital_ids.reshape(PAIR_DEV, 2), offsets], axis=1).astype(jnp.int32)


def draw_pairs(key, part):
    block_keys = jax.vmap(lambda number: jax.random.fold_in(jax.random.fold_in(key, 7717), number))(jnp.arange(N_ORB, dtype=jnp.int32))
    return jax.vmap(pair_block)(block_keys).reshape(NPAIRS, 4)


def draw_tiles(key, part):
    keys = jax.random.split(jax.random.fold_in(key, 3301), 2)
    row_block = jax.random.randint(keys[0], (NTILES,), 0, N_ORB)
    stride = jax.random.randint(keys[1], (NTILES,), 1, N_ORB)
    col_block = (row_block + stride) % N_ORB
    return jnp.stack([row_block, col_block], axis=1).astype(jnp.int32)


def steps_of(stream_key, shape, cuts, least, high):
    def one(axis_at, parts):
        heights = jax.random.uniform(jax.random.fold_in(jax.random.fold_in(stream_key, 6), axis_at), (parts,), jnp.float32, least / len(cuts), high / len(cuts))
        return jnp.repeat(jnp.exp(heights), shape[axis_at] // parts).reshape((-1,) + (1,) * (len(shape) - axis_at - 1))

    loudness = one(*cuts[0])
    for cut in cuts[1:]:
        loudness = loudness * one(*cut)
    return loudness


def centred(stream_key, shape, width, limit, shards=(), kind=jnp.bfloat16):
    level = steps_of(stream_key, shape, shards, -0.22, 0.18) if shards else 1.0
    drawn = jax.random.normal(stream_key, shape, jnp.float32) * width * level
    return jnp.minimum(jnp.maximum(drawn, -limit), limit).astype(kind)


def setup_inputs(seed: int = 0) -> dict:
    streams_of = jax.random.split(jax.random.key(seed), 4)
    return {
        "orbitals": centred(streams_of[0], (NORB, BOX, BOX * BOX), 1.0, 6.0, ((0, 32),)),
        "pairs": draw_pairs(jax.random.fold_in(streams_of[3], 71), 0),
        "tiles": draw_tiles(jax.random.fold_in(streams_of[3], 71), 0),
    }


SCREENING = 0.02
MIXING = 0.25


def neighbours(padded_x, field_in):
    beside = padded_x[..., 2:, :] + padded_x[..., :-2, :]
    zero_rows = jnp.zeros(field_in.shape[:-1] + (BOX,), jnp.float32)
    beside = beside + jnp.concatenate([field_in[..., BOX:], zero_rows], axis=-1)
    beside = beside + jnp.concatenate([zero_rows, field_in[..., :-BOX]], axis=-1)
    column = jnp.arange(BOX * BOX, dtype=jnp.int32) % BOX
    zero_cells = jnp.zeros(field_in.shape[:-1] + (1,), jnp.float32)
    upward = jnp.concatenate([field_in[..., 1:], zero_cells], axis=-1)
    downward = jnp.concatenate([zero_cells, field_in[..., :-1]], axis=-1)
    beside = beside + jnp.where(column < BOX - 1, upward, 0.0) + jnp.where(column > 0, downward, 0.0)
    return (6.0 + SCREENING) * field_in - beside


def operate_box(field_in):
    padded = jnp.pad(field_in, ((1, 1), (0, 0)))
    return neighbours(padded, field_in)


def chebyshev(density, operate):
    center = 6.0 + SCREENING
    radius = 6.0
    ratio = center / radius
    residual = density
    direction = density / center
    solution = direction
    previous = 1.0 / ratio
    for sweep_index in range(SWEEPS):
        residual = residual - operate(direction)
        current = 1.0 / (2.0 * ratio - previous)
        direction = (current * previous) * direction + (2.0 * current / radius) * residual
        solution = solution + direction
        previous = current
    return solution


def move(field_in, offset_y, offset_z):
    cells = jnp.arange(BOX * BOX, dtype=jnp.int32)
    row_index = cells // BOX + offset_y
    col_index = cells % BOX + offset_z
    valid = (row_index >= 0) & (row_index < BOX) & (col_index >= 0) & (col_index < BOX)
    rolled = jnp.roll(field_in, -(offset_y * BOX + offset_z), axis=-1)
    return jnp.where(valid, rolled, 0.0)


def own_product(operands):
    return jnp.sum(operands[0].astype(jnp.float32) * operands[1].astype(jnp.float32))


def reference(orbitals, pairs, tiles):
    def accumulate(forces, pair_row):
        first_box = lax.dynamic_index_in_dim(orbitals, pair_row[0], 0, keepdims=False).astype(jnp.float32)
        second_box = lax.dynamic_index_in_dim(orbitals, pair_row[1], 0, keepdims=False).astype(jnp.float32)
        shifted = move(second_box, pair_row[2], pair_row[3])
        potential = chebyshev(first_box * shifted, operate_box)
        to_first = -MIXING * potential * shifted
        to_second = -MIXING * move(potential * first_box, -pair_row[2], -pair_row[3])
        forces = forces.at[pair_row[0]].add(to_first)
        forces = forces.at[pair_row[1]].add(to_second)
        return forces, None

    forces = lax.scan(accumulate, jnp.zeros(orbitals.shape, jnp.float32), pairs)[0]
    rounded = forces.astype(jnp.bfloat16)
    self_intersection = lax.map(own_product, (orbitals.reshape(NORB, -1), rounded.reshape(NORB, -1)))
    self_intersection = self_intersection * (BOX ** -2.5)
    intersection = lax.dot_general(orbitals.reshape(NORB, -1), rounded.reshape(NORB, -1),
                              (((1,), (1,)), ((), ())), preferred_element_type=jnp.float32)
    blocks = intersection.reshape(N_ORB, ORB_DEV, N_ORB, ORB_DEV).transpose(0, 2, 1, 3)
    blocks = blocks.reshape(N_ORB * N_ORB, ORB_DEV * ORB_DEV)
    picked = jnp.take(blocks, tiles[:, 0] * N_ORB + tiles[:, 1], axis=0)
    return forces, picked * (BOX ** -1.5), self_intersection
```

```python
import functools

import jax
import jax.numpy as jnp
import numpy as np
from jax import lax
from jax.experimental import pallas as pl
from jax.experimental.pallas import tpu as pltpu
from jax.sharding import PartitionSpec as P

BOX = 64
SWEEPS = 3
SHIFT = 16
LANES = 128

SCREENING = 0.02
MIXING = 0.25


def padded_2(array, sides, width):
    for axis, dim in sides:
        devices, length = (lax.axis_size(axis), array.shape[dim])
        up = [(i, (i + 1) % devices) for i in range(devices - 1)]
        down = [(j, i) for i, j in up]
        last = lax.slice_in_dim(array, length - width, length, axis=dim)
        first = lax.slice_in_dim(array, 0, width, axis=dim)
        before = lax.ppermute(last, axis, up)
        after = lax.ppermute(first, axis, down)
        array = jnp.concatenate([before, array, after], axis=dim)
    return array


def operate_slab(field_in):
    padded = padded_2(field_in, (("grid", 1),), 1)
    beside = padded[:, 2:, :] + padded[:, :-2, :]
    zero_rows = jnp.zeros(field_in.shape[:-1] + (BOX,), jnp.float32)
    beside = beside + jnp.concatenate([field_in[..., BOX:], zero_rows], axis=-1)
    beside = beside + jnp.concatenate([zero_rows, field_in[..., :-BOX]], axis=-1)
    column = jnp.arange(BOX * BOX, dtype=jnp.int32) % BOX
    zero_cells = jnp.zeros(field_in.shape[:-1] + (1,), jnp.float32)
    upward = jnp.concatenate([field_in[..., 1:], zero_cells], axis=-1)
    downward = jnp.concatenate([zero_cells, field_in[..., :-1]], axis=-1)
    beside = (
        beside + jnp.where(column < BOX - 1, upward, 0.0) + jnp.where(column > 0, downward, 0.0)
    )
    return (6.0 + SCREENING) * field_in - beside


def chebyshev(density):
    center = 6.0 + SCREENING
    radius = 6.0
    ratio = center / radius
    residual = density
    direction = density / center
    solution = direction
    previous = 1.0 / ratio
    for sweep_index in range(SWEEPS):
        residual = residual - operate_slab(direction)
        current = 1.0 / (2.0 * ratio - previous)
        direction = current * previous * direction + 2.0 * current / radius * residual
        solution = solution + direction
        previous = current
    return solution


def move(field_in, offset_y, offset_z):
    cells = jnp.arange(BOX * BOX, dtype=jnp.int32)
    row_index = cells // BOX + offset_y
    col_index = cells % BOX + offset_z
    valid = (row_index >= 0) & (row_index < BOX) & (col_index >= 0) & (col_index < BOX)
    rolled = jnp.roll(field_in, -(offset_y * BOX + offset_z), axis=-1)
    return jnp.where(valid, rolled, 0.0)


def general_body(orbitals, pairs, tiles):
    n_orb = lax.axis_size("orb")
    orb_dev, planes, flat_cells = orbitals.shape
    pair_count = pairs.shape[0]
    ref_count = 2 * pair_count
    ref_orb = pairs[:, :2].reshape(ref_count)
    owner_index = ref_orb // orb_dev
    local_index = ref_orb % orb_dev
    capacity = (2 * pair_count + n_orb - 1) // n_orb + 1
    same_owner = owner_index[:, None] == owner_index[None, :]
    earlier = jnp.arange(ref_count)[None, :] < jnp.arange(ref_count)[:, None]
    slot_index = jnp.sum(same_owner & earlier, axis=1)
    target = owner_index * capacity + slot_index
    positions = jnp.arange(n_orb * capacity, dtype=jnp.int32)
    placed = target[None, :] == positions[:, None]
    request = jnp.max(jnp.where(placed, local_index[None, :], 0), axis=1).reshape(n_orb, capacity)
    asked = lax.all_to_all(request, "orb", split_axis=0, concat_axis=0, tiled=True)
    outgoing = jnp.take(orbitals, asked.reshape(-1), axis=0).reshape(
        n_orb, capacity, planes, flat_cells
    )
    incoming = lax.all_to_all(outgoing, "orb", split_axis=0, concat_axis=0, tiled=True)
    fetched = jnp.take(incoming.reshape(n_orb * capacity, planes, flat_cells), target, axis=0)
    fetched = fetched.reshape(pair_count, 2, planes, flat_cells)
    first_box = fetched[:, 0].astype(jnp.float32)
    second_box = fetched[:, 1].astype(jnp.float32)
    offset_y = pairs[:, 2]
    offset_z = pairs[:, 3]
    shifted = jax.vmap(move)(second_box, offset_y, offset_z)
    potential = chebyshev(first_box * shifted)
    to_first = -MIXING * potential * shifted
    to_second = -MIXING * jax.vmap(move)(potential * first_box, -offset_y, -offset_z)
    contrib = jnp.stack([to_first, to_second], axis=1).reshape(ref_count, planes * flat_cells)
    sending = jnp.dot(placed.astype(jnp.float32), contrib, precision=lax.Precision.HIGHEST)
    returned = lax.all_to_all(
        sending.reshape(n_orb, capacity, planes * flat_cells),
        "orb",
        split_axis=0,
        concat_axis=0,
        tiled=True,
    )
    owned = (asked.reshape(-1)[None, :] == jnp.arange(orb_dev, dtype=jnp.int32)[:, None]).astype(
        jnp.float32
    )
    exch_force = jnp.dot(
        owned,
        returned.reshape(n_orb * capacity, planes * flat_cells),
        precision=lax.Precision.HIGHEST,
    )
    rounded = exch_force.astype(jnp.bfloat16)
    own_rows = orbitals.reshape(orb_dev, planes * flat_cells)
    self_part = jnp.einsum("kc,kc->k", own_rows, rounded, preferred_element_type=jnp.float32)
    self_intersection = lax.psum(self_part, "grid") * BOX ** (-2.5)
    orbital_rows, force_rows = (
        lax.all_to_all(own_rows, "orb", split_axis=1, concat_axis=0, tiled=True),
        lax.all_to_all(rounded, "orb", split_axis=1, concat_axis=0, tiled=True),
    )
    intersection = lax.dot_general(
        orbital_rows, force_rows, (((1,), (1,)), ((), ())), preferred_element_type=jnp.float32
    )
    blocks = intersection.reshape(n_orb, orb_dev, n_orb, orb_dev).transpose(0, 2, 1, 3)
    blocks = blocks.reshape(n_orb * n_orb, orb_dev * orb_dev)
    picked = jnp.take(blocks, tiles[:, 0] * n_orb + tiles[:, 1], axis=0)
    summed = lax.psum_scatter(picked, ("grid", "orb"), scatter_dimension=0, tiled=True)
    return (
        exch_force.reshape(orb_dev, planes, flat_cells),
        summed * BOX ** (-1.5),
        self_intersection,
    )


def polynomial():
    center = 6.0 + SCREENING
    radius = 6.0
    ratio = center / radius
    residual = np.zeros(SWEEPS + 1)
    residual[0] = 1.0
    direction = residual / center
    total = direction.copy()
    previous = 1.0 / ratio
    for _ in range(SWEEPS):
        moved = np.concatenate([[0.0], direction[:-1]])
        residual = residual - (center * direction - moved)
        current = 1.0 / (2.0 * ratio - previous)
        direction = current * previous * direction + 2.0 * current / radius * residual
        total = total + direction
        previous = current
    return [-MIXING * float(value) for value in total]


def chain(n_orb):
    if n_orb % 8:
        return list(range(n_orb))
    order = []
    for layer in range(n_orb // 8):
        ring = [0, 1, 3, 2]
        for chip in ring if layer % 2 == 0 else ring[::-1]:
            order += [(layer * 4 + chip) * 2, (layer * 4 + chip) * 2 + 1]
    return order


PAD = 16


def shift_cells(field_in, offset_y, offset_z, pad):
    planes, rows, lanes = field_in.shape
    step = offset_y * BOX + offset_z
    down = lax.shift_right_arithmetic(step, jnp.int32(7))
    along = step - down * lanes
    turned = pltpu.roll(field_in.reshape(planes * rows, lanes), lax.rem(lanes - along, lanes), 1)
    pad[:, PAD:PAD + rows, :] = turned.reshape(planes, rows, lanes)
    near = pad[:, pl.ds(PAD + down, rows), :]
    far = pad[:, pl.ds(PAD + 1 + down, rows), :]
    lane = lax.broadcasted_iota(jnp.int32, (rows, lanes), 1)
    column = lax.rem(lane, BOX) + offset_z
    valid = (column >= 0) & (column < BOX)
    keep = valid & (lane < lanes - along)
    other = valid & (lane >= lanes - along)
    return jnp.where(keep[None], near, jnp.where(other[None], far, 0.0))


def density_kernel(refs, slab, out, pad):
    pad[...] = jnp.zeros_like(pad)

    def pair(p, carry):
        first = slab[refs[p, 0]].astype(jnp.float32)
        second = slab[refs[p, 1]].astype(jnp.float32)
        out[p] = (first * shift_cells(second, refs[p, 2], refs[p, 3], pad)).astype(out.dtype)
        return carry

    lax.fori_loop(0, out.shape[0], pair, 0)


def force_kernel(n_orb, before, coefficients, refs, place, slab, *rest):
    sides = rest[:-4]
    rounded, forces, pad, pad_back = rest[-4:]
    orbitals, planes, rows, lanes = slab.shape
    pad[...] = jnp.zeros_like(pad)
    pad_back[...] = jnp.zeros_like(pad_back)

    def clear(k, carry):
        forces[k] = jnp.zeros(forces.shape[1:], jnp.float32)
        return carry

    lax.fori_loop(0, orbitals, clear, 0)
    first_plane = place[0] * planes
    lane = lax.broadcasted_iota(jnp.int32, (rows, lanes), 1)
    row = lax.broadcasted_iota(jnp.int32, (rows, lanes), 0)
    low_half = lane < BOX
    column = lax.rem(lane, BOX)
    not_last = column < BOX - 1
    not_first = column > 0
    inner = jnp.where(low_half, jnp.where(row > 0, 1.0, 0.0), jnp.where(row < rows - 1, 1.0, 0.0))
    inside = []
    for k in range(planes + 2 * SWEEPS):
        x = first_plane + (k - SWEEPS)
        inside.append(jnp.where((x >= 0) & (x < n_orb * planes), 1.0, 0.0).astype(jnp.float32))

    def in_plane(field_in):
        swapped = pltpu.roll(field_in, BOX, 1)
        across = jnp.where(low_half, pltpu.roll(swapped, 1, 0), pltpu.roll(swapped, rows - 1, 0))
        upward = jnp.where(not_last, pltpu.roll(field_in, lanes - 1, 1), 0.0)
        downward = jnp.where(not_first, pltpu.roll(field_in, 1, 1), 0.0)
        return swapped + across * inner + upward + downward

    def pair(p, carry):
        first_at, second_at, offset_y, offset_z = refs[p, 0], refs[p, 1], refs[p, 2], refs[p, 3]
        first = slab[first_at].astype(jnp.float32)
        shifted = shift_cells(slab[second_at].astype(jnp.float32), offset_y, offset_z, pad)
        own = first * shifted
        density = []
        for ref, plane in before[0]:
            density.append(sides[ref][p, plane].astype(jnp.float32))
        density += [own[k] for k in range(planes)]
        for ref, plane in before[1]:
            density.append(sides[ref][p, plane].astype(jnp.float32))
        field = [coefficients[SWEEPS] * d for d in density]
        for sweep in range(SWEEPS):
            factor = coefficients[SWEEPS - 1 - sweep]
            low, high = sweep + 1, planes + 2 * SWEEPS - 1 - sweep
            after = [None] * len(field)
            for k in range(low, high):
                value = factor * density[k] + (field[k - 1] + field[k + 1] + in_plane(field[k]))
                if k < SWEEPS or k >= SWEEPS + planes:
                    value = value * inside[k]
                after[k] = value
            field = after
        potential = jnp.stack(field[SWEEPS:SWEEPS + planes])
        forces[first_at] += potential * shifted
        forces[second_at] += shift_cells(potential * first, -offset_y, -offset_z, pad_back)
        return carry

    lax.fori_loop(0, refs.shape[0], pair, 0)

    def finish(k, carry):
        rounded[k] = forces[k].astype(rounded.dtype)
        return carry

    lax.fori_loop(0, orbitals, finish, 0)


def slab_body(orbitals, pairs, tiles):
    n_orb = lax.axis_size("orb")
    orb_dev, box_planes, flat_cells = orbitals.shape
    planes = box_planes // n_orb
    rows = flat_cells // LANES
    n_orbitals = n_orb * orb_dev
    order = chain(n_orb)
    position = [order.index(d) for d in range(n_orb)]
    groups = [order]
    exchange = functools.partial(
        lax.all_to_all, axis_name="orb", split_axis=0, concat_axis=0, tiled=True,
        axis_index_groups=groups,
    )
    seat = jnp.asarray(position, jnp.int32)
    me = lax.axis_index("orb")

    leaving = orbitals.reshape(orb_dev, n_orb, planes, rows, LANES).transpose(1, 0, 2, 3, 4)
    slab = exchange(leaving).reshape(n_orbitals, planes, rows, LANES)
    every = exchange(jnp.broadcast_to(pairs[None], (n_orb,) + pairs.shape)).reshape(-1, 4)
    ids = every[:, :2]
    slots = jnp.take(seat, ids // orb_dev) * orb_dev + ids % orb_dev
    refs = jnp.concatenate([slots, every[:, 2:]], axis=1)
    n_pairs = refs.shape[0]

    vmem = pl.BlockSpec(memory_space=pltpu.VMEM)
    smem = pl.BlockSpec(memory_space=pltpu.SMEM)
    limit = pltpu.CompilerParams(vmem_limit_bytes=60 * 1024 * 1024)
    pad = pltpu.VMEM((planes, rows + 2 * PAD, LANES), jnp.float32)
    density = pl.pallas_call(
        density_kernel,
        out_shape=jax.ShapeDtypeStruct((n_pairs, planes, rows, LANES), jnp.bfloat16),
        in_specs=[smem, vmem],
        out_specs=vmem,
        scratch_shapes=[pad],
        compiler_params=limit,
    )(refs, slab)

    sides, lower, upper = [], [], []
    left = SWEEPS
    hop = 1
    while left > 0:
        width = min(planes, left)
        up = [(order[s], order[s + hop]) for s in range(n_orb - hop)]
        down = [(j, i) for i, j in up]
        sides.append(lax.ppermute(density[:, planes - width:], "orb", up))
        lower = [(len(sides) - 1, k) for k in range(width)] + lower
        sides.append(lax.ppermute(density[:, :width], "orb", down))
        upper = upper + [(len(sides) - 1, k) for k in range(width)]
        left -= width
        hop += 1

    rounded = pl.pallas_call(
        functools.partial(force_kernel, n_orb, (lower, upper), polynomial()),
        out_shape=jax.ShapeDtypeStruct((n_orbitals, planes, rows, LANES), jnp.bfloat16),
        in_specs=[smem, smem, vmem] + [vmem] * len(sides),
        out_specs=vmem,
        scratch_shapes=[
            pltpu.VMEM((n_orbitals, planes, rows, LANES), jnp.float32), pad, pad,
        ],
        compiler_params=limit,
    )(refs, jnp.take(seat, me).reshape(1), slab, *sides)

    returned = exchange(rounded.reshape(n_orb, orb_dev, planes, rows, LANES))
    exch_force = returned.astype(jnp.float32).transpose(1, 0, 2, 3, 4)
    exch_force = exch_force.reshape(orb_dev, box_planes, flat_cells)

    intersection = lax.dot_general(
        slab.reshape(n_orbitals, -1), rounded.reshape(n_orbitals, -1),
        (((1,), (1,)), ((), ())), preferred_element_type=jnp.float32,
    )
    self_part = jnp.diagonal(intersection).reshape(n_orb, orb_dev)
    blocks = intersection.reshape(n_orb, orb_dev, n_orb, orb_dev).transpose(0, 2, 1, 3)
    blocks = blocks.reshape(n_orb * n_orb, orb_dev * orb_dev)
    chosen = jnp.take(seat, tiles[:, 0]) * n_orb + jnp.take(seat, tiles[:, 1])
    picked = jnp.take(blocks, chosen, axis=0).reshape(n_orb, -1)
    parts = jnp.concatenate([jnp.take(picked, np.asarray(order), axis=0), self_part], axis=1)
    summed = jnp.sum(exchange(parts), axis=0)
    width = picked.shape[1]
    tile_rows = summed[:width].reshape(-1, orb_dev * orb_dev)
    return exch_force, tile_rows * BOX ** (-1.5), summed[width:] * BOX ** (-2.5)


def body(orbitals, pairs, tiles):
    planes, flat_cells = orbitals.shape[1:]
    n_orb = lax.axis_size("orb")
    if lax.axis_size("grid") == 1 and planes % n_orb == 0 and flat_cells % LANES == 0:
        return slab_body(orbitals, pairs, tiles)
    return general_body(orbitals, pairs, tiles)


def solution(mesh):
    in_specs = (P("orb", "grid", None), P("orb", None), P())
    out_specs = (P("orb", "grid", None), P(("grid", "orb"), None), P("orb"))
    return jax.shard_map(body, mesh=mesh, in_specs=in_specs, out_specs=out_specs, check_vma=False)
```

```python
import functools
import math

import jax
import jax.numpy as jnp
import numpy as np
from jax import lax
from jax.experimental import pallas as pl
from jax.experimental.pallas import tpu as pltpu
from jax.sharding import PartitionSpec as P

BOX = 64
SWEEPS = 3
SHIFT = 16
LANES = 128

SCREENING = 0.02
MIXING = 0.25


def padded_2(array, sides, width):
    for axis, dim in sides:
        devices, length = (lax.axis_size(axis), array.shape[dim])
        up = [(i, (i + 1) % devices) for i in range(devices - 1)]
        down = [(j, i) for i, j in up]
        last = lax.slice_in_dim(array, length - width, length, axis=dim)
        first = lax.slice_in_dim(array, 0, width, axis=dim)
        before = lax.ppermute(last, axis, up)
        after = lax.ppermute(first, axis, down)
        array = jnp.concatenate([before, array, after], axis=dim)
    return array


def operate_slab(field_in):
    padded = padded_2(field_in, (("grid", 1),), 1)
    beside = padded[:, 2:, :] + padded[:, :-2, :]
    zero_rows = jnp.zeros(field_in.shape[:-1] + (BOX,), jnp.float32)
    beside = beside + jnp.concatenate([field_in[..., BOX:], zero_rows], axis=-1)
    beside = beside + jnp.concatenate([zero_rows, field_in[..., :-BOX]], axis=-1)
    column = jnp.arange(BOX * BOX, dtype=jnp.int32) % BOX
    zero_cells = jnp.zeros(field_in.shape[:-1] + (1,), jnp.float32)
    upward = jnp.concatenate([field_in[..., 1:], zero_cells], axis=-1)
    downward = jnp.concatenate([zero_cells, field_in[..., :-1]], axis=-1)
    beside = (
        beside + jnp.where(column < BOX - 1, upward, 0.0) + jnp.where(column > 0, downward, 0.0)
    )
    return (6.0 + SCREENING) * field_in - beside


def chebyshev(density):
    center = 6.0 + SCREENING
    radius = 6.0
    ratio = center / radius
    residual = density
    direction = density / center
    solution = direction
    previous = 1.0 / ratio
    for sweep_index in range(SWEEPS):
        residual = residual - operate_slab(direction)
        current = 1.0 / (2.0 * ratio - previous)
        direction = current * previous * direction + 2.0 * current / radius * residual
        solution = solution + direction
        previous = current
    return solution


def move(field_in, offset_y, offset_z):
    cells = jnp.arange(BOX * BOX, dtype=jnp.int32)
    row_index = cells // BOX + offset_y
    col_index = cells % BOX + offset_z
    valid = (row_index >= 0) & (row_index < BOX) & (col_index >= 0) & (col_index < BOX)
    rolled = jnp.roll(field_in, -(offset_y * BOX + offset_z), axis=-1)
    return jnp.where(valid, rolled, 0.0)


def general_body(orbitals, pairs, tiles):
    n_orb = lax.axis_size("orb")
    orb_dev, planes, flat_cells = orbitals.shape
    pair_count = pairs.shape[0]
    ref_count = 2 * pair_count
    ref_orb = pairs[:, :2].reshape(ref_count)
    owner_index = ref_orb // orb_dev
    local_index = ref_orb % orb_dev
    capacity = (2 * pair_count + n_orb - 1) // n_orb + 1
    same_owner = owner_index[:, None] == owner_index[None, :]
    earlier = jnp.arange(ref_count)[None, :] < jnp.arange(ref_count)[:, None]
    slot_index = jnp.sum(same_owner & earlier, axis=1)
    target = owner_index * capacity + slot_index
    positions = jnp.arange(n_orb * capacity, dtype=jnp.int32)
    placed = target[None, :] == positions[:, None]
    request = jnp.max(jnp.where(placed, local_index[None, :], 0), axis=1).reshape(n_orb, capacity)
    asked = lax.all_to_all(request, "orb", split_axis=0, concat_axis=0, tiled=True)
    outgoing = jnp.take(orbitals, asked.reshape(-1), axis=0).reshape(
        n_orb, capacity, planes, flat_cells
    )
    incoming = lax.all_to_all(outgoing, "orb", split_axis=0, concat_axis=0, tiled=True)
    fetched = jnp.take(incoming.reshape(n_orb * capacity, planes, flat_cells), target, axis=0)
    fetched = fetched.reshape(pair_count, 2, planes, flat_cells)
    first_box = fetched[:, 0].astype(jnp.float32)
    second_box = fetched[:, 1].astype(jnp.float32)
    offset_y = pairs[:, 2]
    offset_z = pairs[:, 3]
    shifted = jax.vmap(move)(second_box, offset_y, offset_z)
    potential = chebyshev(first_box * shifted)
    to_first = -MIXING * potential * shifted
    to_second = -MIXING * jax.vmap(move)(potential * first_box, -offset_y, -offset_z)
    contrib = jnp.stack([to_first, to_second], axis=1).reshape(ref_count, planes * flat_cells)
    sending = jnp.dot(placed.astype(jnp.float32), contrib, precision=lax.Precision.HIGHEST)
    returned = lax.all_to_all(
        sending.reshape(n_orb, capacity, planes * flat_cells),
        "orb",
        split_axis=0,
        concat_axis=0,
        tiled=True,
    )
    owned = (asked.reshape(-1)[None, :] == jnp.arange(orb_dev, dtype=jnp.int32)[:, None]).astype(
        jnp.float32
    )
    exch_force = jnp.dot(
        owned,
        returned.reshape(n_orb * capacity, planes * flat_cells),
        precision=lax.Precision.HIGHEST,
    )
    rounded = exch_force.astype(jnp.bfloat16)
    own_rows = orbitals.reshape(orb_dev, planes * flat_cells)
    self_part = jnp.einsum("kc,kc->k", own_rows, rounded, preferred_element_type=jnp.float32)
    self_intersection = lax.psum(self_part, "grid") * BOX ** (-2.5)
    orbital_rows, force_rows = (
        lax.all_to_all(own_rows, "orb", split_axis=1, concat_axis=0, tiled=True),
        lax.all_to_all(rounded, "orb", split_axis=1, concat_axis=0, tiled=True),
    )
    intersection = lax.dot_general(
        orbital_rows, force_rows, (((1,), (1,)), ((), ())), preferred_element_type=jnp.float32
    )
    blocks = intersection.reshape(n_orb, orb_dev, n_orb, orb_dev).transpose(0, 2, 1, 3)
    blocks = blocks.reshape(n_orb * n_orb, orb_dev * orb_dev)
    picked = jnp.take(blocks, tiles[:, 0] * n_orb + tiles[:, 1], axis=0)
    summed = lax.psum_scatter(picked, ("grid", "orb"), scatter_dimension=0, tiled=True)
    return (
        exch_force.reshape(orb_dev, planes, flat_cells),
        summed * BOX ** (-1.5),
        self_intersection,
    )


def polynomial():
    center = 6.0 + SCREENING
    radius = 6.0
    ratio = center / radius
    residual = np.zeros(SWEEPS + 1)
    residual[0] = 1.0
    direction = residual / center
    total = direction.copy()
    previous = 1.0 / ratio
    for _ in range(SWEEPS):
        moved = np.concatenate([[0.0], direction[:-1]])
        residual = residual - (center * direction - moved)
        current = 1.0 / (2.0 * ratio - previous)
        direction = current * previous * direction + 2.0 * current / radius * residual
        total = total + direction
        previous = current
    return [-MIXING * float(value) for value in total]


def chain(n_orb):
    if n_orb % 8:
        return list(range(n_orb))
    order = []
    for layer in range(n_orb // 8):
        ring = [0, 1, 3, 2]
        for chip in ring if layer % 2 == 0 else ring[::-1]:
            order += [(layer * 4 + chip) * 2, (layer * 4 + chip) * 2 + 1]
    return order


PAD = 16


def shift_cells(field_in, offset_y, offset_z, pad):
    planes, rows, lanes = field_in.shape
    step = offset_y * BOX + offset_z
    down = lax.shift_right_arithmetic(step, jnp.int32(7))
    along = step - down * lanes
    turned = pltpu.roll(field_in.reshape(planes * rows, lanes), lax.rem(lanes - along, lanes), 1)
    pad[:, PAD:PAD + rows, :] = turned.reshape(planes, rows, lanes)
    near = pad[:, pl.ds(PAD + down, rows), :]
    far = pad[:, pl.ds(PAD + 1 + down, rows), :]
    lane = lax.broadcasted_iota(jnp.int32, (rows, lanes), 1)
    column = lax.rem(lane, BOX) + offset_z
    valid = (column >= 0) & (column < BOX)
    keep = valid & (lane < lanes - along)
    other = valid & (lane >= lanes - along)
    return jnp.where(keep[None], near, jnp.where(other[None], far, 0.0))


def density_kernel(refs, slab, out, pads):
    pads[...] = jnp.zeros_like(pads)
    width = pads.shape[0]

    def group(g, carry):
        values = []
        for u in range(width):
            p = g * width + u
            first = slab[refs[p, 0]].astype(jnp.float32)
            second = slab[refs[p, 1]].astype(jnp.float32)
            values.append(first * shift_cells(second, refs[p, 2], refs[p, 3], pads.at[u]))
        for u in range(width):
            out[g * width + u] = values[u].astype(out.dtype)
        return carry

    lax.fori_loop(0, out.shape[0] // width, group, 0)


def spread_kernel(own, out, lines):
    box_planes, flat_cells = own.shape[1:]
    slabs, _, planes, rows, lanes = out.shape
    for r in range(rows):
        lines[pl.ds(r, box_planes, stride=rows), :] = own[0, :, r * lanes:(r + 1) * lanes].astype(
            jnp.float32
        )
    out[...] = lines[...].reshape(out.shape).astype(out.dtype)


def collect_kernel(back, out, lines):
    box_planes, flat_cells = out.shape[1:]
    slabs, _, planes, rows, lanes = back.shape
    lines[...] = back[...].astype(jnp.float32).reshape(lines.shape)
    for r in range(rows):
        out[0, :, r * lanes:(r + 1) * lanes] = lines[pl.ds(r, box_planes, stride=rows), :]


def force_kernel(n_orb, before, coefficients, last, refs, place, slab, *rest):
    if last:
        sides = rest[:-6]
        all_refs, earlier, rounded, forces, pads, pads_back = rest[-6:]
    else:
        sides = rest[:-3]
        given, pads, pads_back = rest[-3:]
    orbitals, planes, rows, lanes = slab.shape
    width = pads.shape[0]
    pads[...] = jnp.zeros_like(pads)
    pads_back[...] = jnp.zeros_like(pads_back)

    if last:
        def clear(k, carry):
            forces[k] = jnp.zeros(forces.shape[1:], jnp.float32)
            return carry

        lax.fori_loop(0, orbitals, clear, 0)

        def add(p, carry):
            forces[all_refs[p, 0]] += earlier[p, 0]
            forces[all_refs[p, 1]] += earlier[p, 1]
            return carry

        lax.fori_loop(0, earlier.shape[0], add, 0)

    first_plane = place[0] * planes
    lane = lax.broadcasted_iota(jnp.int32, (rows, lanes), 1)
    row = lax.broadcasted_iota(jnp.int32, (rows, lanes), 0)
    low_half = lane < BOX
    column = lax.rem(lane, BOX)
    not_last = column < BOX - 1
    not_first = column > 0
    inner = jnp.where(low_half, jnp.where(row > 0, 1.0, 0.0), jnp.where(row < rows - 1, 1.0, 0.0))
    inside = []
    for k in range(planes + 2 * SWEEPS):
        x = first_plane + (k - SWEEPS)
        inside.append(jnp.where((x >= 0) & (x < n_orb * planes), 1.0, 0.0).astype(jnp.float32))

    def in_plane(field_in):
        swapped = pltpu.roll(field_in, BOX, 1)
        across = jnp.where(low_half, pltpu.roll(swapped, 1, 0), pltpu.roll(swapped, rows - 1, 0))
        upward = jnp.where(not_last, pltpu.roll(field_in, lanes - 1, 1), 0.0)
        downward = jnp.where(not_first, pltpu.roll(field_in, 1, 1), 0.0)
        return swapped + across * inner + upward + downward

    def contributions(p, pad, pad_back):
        first_at, second_at, offset_y, offset_z = refs[p, 0], refs[p, 1], refs[p, 2], refs[p, 3]
        first = slab[first_at].astype(jnp.float32)
        shifted = shift_cells(slab[second_at].astype(jnp.float32), offset_y, offset_z, pad)
        own = first * shifted
        density = []
        for ref, plane in before[0]:
            density.append(sides[ref][p, plane].astype(jnp.float32))
        density += [own[k] for k in range(planes)]
        for ref, plane in before[1]:
            density.append(sides[ref][p, plane].astype(jnp.float32))
        field = [coefficients[SWEEPS] * d for d in density]
        for sweep in range(SWEEPS):
            factor = coefficients[SWEEPS - 1 - sweep]
            low, high = sweep + 1, planes + 2 * SWEEPS - 1 - sweep
            after = [None] * len(field)
            for k in range(low, high):
                value = factor * density[k] + (field[k - 1] + field[k + 1] + in_plane(field[k]))
                if k < SWEEPS or k >= SWEEPS + planes:
                    value = value * inside[k]
                after[k] = value
            field = after
        potential = jnp.stack(field[SWEEPS:SWEEPS + planes])
        moved = shift_cells(potential * first, -offset_y, -offset_z, pad_back)
        return potential * shifted, moved

    def group(g, carry):
        pieces = []
        for u in range(width):
            pieces.append(contributions(g * width + u, pads.at[u], pads_back.at[u]))
        for u in range(width):
            p = g * width + u
            if last:
                forces[refs[p, 0]] += pieces[u][0]
                forces[refs[p, 1]] += pieces[u][1]
            else:
                given[p, 0] = pieces[u][0]
                given[p, 1] = pieces[u][1]
        return carry

    lax.fori_loop(0, refs.shape[0] // width, group, 0)

    if last:
        def finish(k, carry):
            rounded[k] = forces[k].astype(rounded.dtype)
            return carry

        lax.fori_loop(0, orbitals, finish, 0)


def reduce_parts(parts, n_orb, me):
    if n_orb & (n_orb - 1):
        return jnp.sum(
            lax.all_to_all(parts, "orb", split_axis=0, concat_axis=0, tiled=True), axis=0
        )
    bit = n_orb // 2
    while bit:
        upper = (me & bit) != 0
        low, high = parts[:bit], parts[bit:]
        sent = jnp.where(upper, low, high)
        kept = jnp.where(upper, high, low)
        parts = kept + lax.ppermute(sent, "orb", [(d, d ^ bit) for d in range(n_orb)])
        bit //= 2
    return parts


def slab_body(orbitals, pairs, tiles):
    n_orb = lax.axis_size("orb")
    orb_dev, box_planes, flat_cells = orbitals.shape
    planes = box_planes // n_orb
    rows = flat_cells // LANES
    n_orbitals = n_orb * orb_dev
    order = chain(n_orb)
    position = [order.index(d) for d in range(n_orb)]
    groups = [order]
    exchange = functools.partial(
        lax.all_to_all, axis_name="orb", split_axis=0, concat_axis=0, tiled=True,
        axis_index_groups=groups,
    )
    seat = jnp.asarray(position, jnp.int32)
    me = lax.axis_index("orb")

    leaving = pl.pallas_call(
        spread_kernel,
        grid=(orb_dev,),
        out_shape=jax.ShapeDtypeStruct((n_orb, orb_dev, planes, rows, LANES), orbitals.dtype),
        in_specs=[pl.BlockSpec((1, box_planes, flat_cells), lambda k: (k, 0, 0))],
        out_specs=pl.BlockSpec((n_orb, 1, planes, rows, LANES), lambda k: (0, k, 0, 0, 0)),
        scratch_shapes=[pltpu.VMEM((box_planes * rows, LANES), jnp.float32)],
    )(orbitals)
    slab = exchange(leaving).reshape(n_orbitals, planes, rows, LANES)
    every = exchange(jnp.broadcast_to(pairs[None], (n_orb,) + pairs.shape)).reshape(-1, 4)
    ids = every[:, :2]
    slots = jnp.take(seat, ids // orb_dev) * orb_dev + ids % orb_dev
    refs = jnp.concatenate([slots, every[:, 2:]], axis=1)
    n_pairs = refs.shape[0]

    vmem = pl.BlockSpec(memory_space=pltpu.VMEM)
    smem = pl.BlockSpec(memory_space=pltpu.SMEM)
    limit = pltpu.CompilerParams(vmem_limit_bytes=58 * 1024 * 1024)
    chunks = 2 if n_pairs % 8 == 0 else 1
    chunk = n_pairs // chunks
    group = math.gcd(chunk, 4)
    pair_group = math.gcd(chunk, 2)

    def pads(count):
        return pltpu.VMEM((count, planes, rows + 2 * PAD, LANES), jnp.float32)

    def density_of(chunk_refs):
        return pl.pallas_call(
            density_kernel,
            out_shape=jax.ShapeDtypeStruct((chunk, planes, rows, LANES), jnp.bfloat16),
            in_specs=[smem, vmem],
            out_specs=vmem,
            scratch_shapes=[pads(group)],
            compiler_params=limit,
            cost_estimate=pl.CostEstimate(
                flops=chunk * 400_000, bytes_accessed=12_000_000, transcendentals=0
            ),
        )(chunk_refs, slab)

    def halo_of(density):
        sides, lower, upper = [], [], []
        left = SWEEPS
        hop = 1
        while left > 0:
            width = min(planes, left)
            up = [(order[s], order[s + hop]) for s in range(n_orb - hop)]
            down = [(j, i) for i, j in up]
            sides.append(lax.ppermute(density[:, planes - width:], "orb", up))
            lower = [(len(sides) - 1, k) for k in range(width)] + lower
            sides.append(lax.ppermute(density[:, :width], "orb", down))
            upper = upper + [(len(sides) - 1, k) for k in range(width)]
            left -= width
            hop += 1
        return sides, (lower, upper)

    place = jnp.take(seat, me).reshape(1)
    chunk_refs = [refs[c * chunk:(c + 1) * chunk] for c in range(chunks)]
    halos = [halo_of(density_of(part)) for part in chunk_refs]
    field_shape = (n_orbitals, planes, rows, LANES)
    given = []
    for c in range(chunks - 1):
        sides, before = halos[c]
        given.append(pl.pallas_call(
            functools.partial(force_kernel, n_orb, before, polynomial(), False),
            out_shape=jax.ShapeDtypeStruct((chunk, 2, planes, rows, LANES), jnp.float32),
            in_specs=[smem, smem, vmem] + [vmem] * len(sides),
            out_specs=vmem,
            scratch_shapes=[pads(pair_group), pads(pair_group)],
            compiler_params=limit,
            cost_estimate=pl.CostEstimate(
                flops=chunk * 2_000_000, bytes_accessed=20_000_000, transcendentals=0
            ),
        )(chunk_refs[c], place, slab, *sides))
    sides, before = halos[-1]
    if given:
        done_refs, done = refs[:(chunks - 1) * chunk], jnp.concatenate(given)
    else:
        done_refs, done = refs[:1], jnp.zeros((1, 2, planes, rows, LANES), jnp.float32)
    rounded = pl.pallas_call(
        functools.partial(force_kernel, n_orb, before, polynomial(), True),
        out_shape=jax.ShapeDtypeStruct(field_shape, jnp.bfloat16),
        in_specs=[smem, smem, vmem] + [vmem] * len(sides) + [smem, vmem],
        out_specs=vmem,
        scratch_shapes=[pltpu.VMEM(field_shape, jnp.float32), pads(pair_group), pads(pair_group)],
        compiler_params=limit,
    )(chunk_refs[-1], place, slab, *sides, done_refs, done)

    returned = exchange(rounded.reshape(n_orb, orb_dev, planes, rows, LANES))
    exch_force = pl.pallas_call(
        collect_kernel,
        grid=(orb_dev,),
        out_shape=jax.ShapeDtypeStruct((orb_dev, box_planes, flat_cells), jnp.float32),
        in_specs=[pl.BlockSpec((n_orb, 1, planes, rows, LANES), lambda k: (0, k, 0, 0, 0))],
        out_specs=pl.BlockSpec((1, box_planes, flat_cells), lambda k: (k, 0, 0)),
        scratch_shapes=[pltpu.VMEM((box_planes * rows, LANES), jnp.float32)],
    )(returned)

    intersection = lax.dot_general(
        slab.reshape(n_orbitals, -1), rounded.reshape(n_orbitals, -1),
        (((1,), (1,)), ((), ())), preferred_element_type=jnp.float32,
    )
    self_part = jnp.diagonal(intersection).reshape(n_orb, orb_dev)
    blocks = intersection.reshape(n_orb, orb_dev, n_orb, orb_dev).transpose(0, 2, 1, 3)
    blocks = blocks.reshape(n_orb * n_orb, orb_dev * orb_dev)
    chosen = jnp.take(seat, tiles[:, 0]) * n_orb + jnp.take(seat, tiles[:, 1])
    picked = jnp.take(blocks, chosen, axis=0).reshape(n_orb, -1)
    parts = jnp.concatenate([picked, jnp.take(self_part, np.asarray(position), axis=0)], axis=1)
    width = picked.shape[1]
    spare = -parts.shape[1] % (8 * LANES)
    parts = jnp.pad(parts, ((0, 0), (0, spare))).reshape(n_orb, -1, LANES)
    summed = reduce_parts(parts, n_orb, me).reshape(-1)
    tile_rows = summed[:width].reshape(-1, orb_dev * orb_dev)
    return exch_force, tile_rows * BOX ** (-1.5), summed[width:width + orb_dev] * BOX ** (-2.5)


def body(orbitals, pairs, tiles):
    planes, flat_cells = orbitals.shape[1:]
    n_orb = lax.axis_size("orb")
    if lax.axis_size("grid") == 1 and planes % n_orb == 0 and flat_cells % LANES == 0:
        return slab_body(orbitals, pairs, tiles)
    return general_body(orbitals, pairs, tiles)


def solution(mesh):
    in_specs = (P("orb", "grid", None), P("orb", None), P())
    out_specs = (P("orb", "grid", None), P(("grid", "orb"), None), P("orb"))
    return jax.shard_map(body, mesh=mesh, in_specs=in_specs, out_specs=out_specs, check_vma=False)
```

```python
import functools
import math

import jax
import jax.numpy as jnp
import numpy as np
from jax import lax
from jax.experimental import pallas as pl
from jax.experimental.pallas import tpu as pltpu
from jax.sharding import PartitionSpec as P

BOX = 64
SWEEPS = 3
SHIFT = 16
LANES = 128

SCREENING = 0.02
MIXING = 0.25


def padded_2(array, sides, width):
    for axis, dim in sides:
        devices, length = (lax.axis_size(axis), array.shape[dim])
        up = [(i, (i + 1) % devices) for i in range(devices - 1)]
        down = [(j, i) for i, j in up]
        last = lax.slice_in_dim(array, length - width, length, axis=dim)
        first = lax.slice_in_dim(array, 0, width, axis=dim)
        before = lax.ppermute(last, axis, up)
        after = lax.ppermute(first, axis, down)
        array = jnp.concatenate([before, array, after], axis=dim)
    return array


def operate_slab(field_in):
    padded = padded_2(field_in, (("grid", 1),), 1)
    beside = padded[:, 2:, :] + padded[:, :-2, :]
    zero_rows = jnp.zeros(field_in.shape[:-1] + (BOX,), jnp.float32)
    beside = beside + jnp.concatenate([field_in[..., BOX:], zero_rows], axis=-1)
    beside = beside + jnp.concatenate([zero_rows, field_in[..., :-BOX]], axis=-1)
    column = jnp.arange(BOX * BOX, dtype=jnp.int32) % BOX
    zero_cells = jnp.zeros(field_in.shape[:-1] + (1,), jnp.float32)
    upward = jnp.concatenate([field_in[..., 1:], zero_cells], axis=-1)
    downward = jnp.concatenate([zero_cells, field_in[..., :-1]], axis=-1)
    beside = (
        beside + jnp.where(column < BOX - 1, upward, 0.0) + jnp.where(column > 0, downward, 0.0)
    )
    return (6.0 + SCREENING) * field_in - beside


def chebyshev(density):
    center = 6.0 + SCREENING
    radius = 6.0
    ratio = center / radius
    residual = density
    direction = density / center
    solution = direction
    previous = 1.0 / ratio
    for sweep_index in range(SWEEPS):
        residual = residual - operate_slab(direction)
        current = 1.0 / (2.0 * ratio - previous)
        direction = current * previous * direction + 2.0 * current / radius * residual
        solution = solution + direction
        previous = current
    return solution


def move(field_in, offset_y, offset_z):
    cells = jnp.arange(BOX * BOX, dtype=jnp.int32)
    row_index = cells // BOX + offset_y
    col_index = cells % BOX + offset_z
    valid = (row_index >= 0) & (row_index < BOX) & (col_index >= 0) & (col_index < BOX)
    rolled = jnp.roll(field_in, -(offset_y * BOX + offset_z), axis=-1)
    return jnp.where(valid, rolled, 0.0)


def general_body(orbitals, pairs, tiles):
    n_orb = lax.axis_size("orb")
    orb_dev, planes, flat_cells = orbitals.shape
    pair_count = pairs.shape[0]
    ref_count = 2 * pair_count
    ref_orb = pairs[:, :2].reshape(ref_count)
    owner_index = ref_orb // orb_dev
    local_index = ref_orb % orb_dev
    capacity = (2 * pair_count + n_orb - 1) // n_orb + 1
    same_owner = owner_index[:, None] == owner_index[None, :]
    earlier = jnp.arange(ref_count)[None, :] < jnp.arange(ref_count)[:, None]
    slot_index = jnp.sum(same_owner & earlier, axis=1)
    target = owner_index * capacity + slot_index
    positions = jnp.arange(n_orb * capacity, dtype=jnp.int32)
    placed = target[None, :] == positions[:, None]
    request = jnp.max(jnp.where(placed, local_index[None, :], 0), axis=1).reshape(n_orb, capacity)
    asked = lax.all_to_all(request, "orb", split_axis=0, concat_axis=0, tiled=True)
    outgoing = jnp.take(orbitals, asked.reshape(-1), axis=0).reshape(
        n_orb, capacity, planes, flat_cells
    )
    incoming = lax.all_to_all(outgoing, "orb", split_axis=0, concat_axis=0, tiled=True)
    fetched = jnp.take(incoming.reshape(n_orb * capacity, planes, flat_cells), target, axis=0)
    fetched = fetched.reshape(pair_count, 2, planes, flat_cells)
    first_box = fetched[:, 0].astype(jnp.float32)
    second_box = fetched[:, 1].astype(jnp.float32)
    offset_y = pairs[:, 2]
    offset_z = pairs[:, 3]
    shifted = jax.vmap(move)(second_box, offset_y, offset_z)
    potential = chebyshev(first_box * shifted)
    to_first = -MIXING * potential * shifted
    to_second = -MIXING * jax.vmap(move)(potential * first_box, -offset_y, -offset_z)
    contrib = jnp.stack([to_first, to_second], axis=1).reshape(ref_count, planes * flat_cells)
    sending = jnp.dot(placed.astype(jnp.float32), contrib, precision=lax.Precision.HIGHEST)
    returned = lax.all_to_all(
        sending.reshape(n_orb, capacity, planes * flat_cells),
        "orb",
        split_axis=0,
        concat_axis=0,
        tiled=True,
    )
    owned = (asked.reshape(-1)[None, :] == jnp.arange(orb_dev, dtype=jnp.int32)[:, None]).astype(
        jnp.float32
    )
    exch_force = jnp.dot(
        owned,
        returned.reshape(n_orb * capacity, planes * flat_cells),
        precision=lax.Precision.HIGHEST,
    )
    rounded = exch_force.astype(jnp.bfloat16)
    own_rows = orbitals.reshape(orb_dev, planes * flat_cells)
    self_part = jnp.einsum("kc,kc->k", own_rows, rounded, preferred_element_type=jnp.float32)
    self_intersection = lax.psum(self_part, "grid") * BOX ** (-2.5)
    orbital_rows, force_rows = (
        lax.all_to_all(own_rows, "orb", split_axis=1, concat_axis=0, tiled=True),
        lax.all_to_all(rounded, "orb", split_axis=1, concat_axis=0, tiled=True),
    )
    intersection = lax.dot_general(
        orbital_rows, force_rows, (((1,), (1,)), ((), ())), preferred_element_type=jnp.float32
    )
    blocks = intersection.reshape(n_orb, orb_dev, n_orb, orb_dev).transpose(0, 2, 1, 3)
    blocks = blocks.reshape(n_orb * n_orb, orb_dev * orb_dev)
    picked = jnp.take(blocks, tiles[:, 0] * n_orb + tiles[:, 1], axis=0)
    summed = lax.psum_scatter(picked, ("grid", "orb"), scatter_dimension=0, tiled=True)
    return (
        exch_force.reshape(orb_dev, planes, flat_cells),
        summed * BOX ** (-1.5),
        self_intersection,
    )


def polynomial():
    center = 6.0 + SCREENING
    radius = 6.0
    ratio = center / radius
    residual = np.zeros(SWEEPS + 1)
    residual[0] = 1.0
    direction = residual / center
    total = direction.copy()
    previous = 1.0 / ratio
    for _ in range(SWEEPS):
        moved = np.concatenate([[0.0], direction[:-1]])
        residual = residual - (center * direction - moved)
        current = 1.0 / (2.0 * ratio - previous)
        direction = current * previous * direction + 2.0 * current / radius * residual
        total = total + direction
        previous = current
    return [-MIXING * float(value) for value in total]


def chain(n_orb):
    if n_orb % 8:
        return list(range(n_orb))
    order = []
    for layer in range(n_orb // 8):
        ring = [0, 1, 3, 2]
        for chip in ring if layer % 2 == 0 else ring[::-1]:
            order += [(layer * 4 + chip) * 2, (layer * 4 + chip) * 2 + 1]
    return order


PAD = 16


def shift_cells(field_in, offset_y, offset_z, pad):
    planes, rows, lanes = field_in.shape
    step = offset_y * BOX + offset_z
    down = lax.shift_right_arithmetic(step, jnp.int32(7))
    along = step - down * lanes
    turned = pltpu.roll(field_in.reshape(planes * rows, lanes), lax.rem(lanes - along, lanes), 1)
    pad[:, PAD:PAD + rows, :] = turned.reshape(planes, rows, lanes)
    near = pad[:, pl.ds(PAD + down, rows), :]
    far = pad[:, pl.ds(PAD + 1 + down, rows), :]
    lane = lax.broadcasted_iota(jnp.int32, (rows, lanes), 1)
    column = lax.rem(lane, BOX) + offset_z
    valid = (column >= 0) & (column < BOX)
    keep = valid & (lane < lanes - along)
    other = valid & (lane >= lanes - along)
    return jnp.where(keep[None], near, jnp.where(other[None], far, 0.0))


def density_kernel(refs, slab, out, pads):
    pads[...] = jnp.zeros_like(pads)
    width = pads.shape[0]

    def group(g, carry):
        values = []
        for u in range(width):
            p = g * width + u
            first = slab[refs[p, 0]].astype(jnp.float32)
            second = slab[refs[p, 1]].astype(jnp.float32)
            values.append(first * shift_cells(second, refs[p, 2], refs[p, 3], pads.at[u]))
        for u in range(width):
            out[g * width + u] = values[u].astype(out.dtype)
        return carry

    lax.fori_loop(0, out.shape[0] // width, group, 0)


def spread_kernel(chosen, own, out, lines):
    box_planes, flat_cells = own.shape[1:]
    slabs, _, planes, rows, lanes = out.shape
    for r in range(rows):
        lines[pl.ds(r, box_planes, stride=rows), :] = own[0, :, r * lanes:(r + 1) * lanes].astype(
            jnp.float32
        )
    out[...] = lines[...].reshape(out.shape).astype(out.dtype)


def orb_count(slots):
    return slots.shape[0] // 2


def collect_kernel(slots, back, out, lines):
    box_planes, flat_cells = out.shape[1:]
    slabs, _, planes, rows, lanes = back.shape
    named = slots[orb_count(slots) + pl.program_id(0)] > 0
    values = back[...].astype(jnp.float32).reshape(lines.shape)
    lines[...] = jnp.where(named, values, 0.0)
    for r in range(rows):
        out[0, :, r * lanes:(r + 1) * lanes] = lines[pl.ds(r, box_planes, stride=rows), :]


def force_kernel(n_orb, before, coefficients, last, refs, place, slab, *rest):
    if last:
        sides = rest[:-6]
        all_refs, earlier, rounded, forces, pads, pads_back = rest[-6:]
    else:
        sides = rest[:-3]
        given, pads, pads_back = rest[-3:]
    orbitals, planes, rows, lanes = slab.shape
    width = pads.shape[0]
    pads[...] = jnp.zeros_like(pads)
    pads_back[...] = jnp.zeros_like(pads_back)

    if last:
        def clear(k, carry):
            forces[k] = jnp.zeros(forces.shape[1:], jnp.float32)
            return carry

        lax.fori_loop(0, orbitals, clear, 0)

        def add(p, carry):
            forces[all_refs[p, 0]] += earlier[p, 0]
            forces[all_refs[p, 1]] += earlier[p, 1]
            return carry

        lax.fori_loop(0, earlier.shape[0], add, 0)

    first_plane = place[0] * planes
    lane = lax.broadcasted_iota(jnp.int32, (rows, lanes), 1)
    row = lax.broadcasted_iota(jnp.int32, (rows, lanes), 0)
    low_half = lane < BOX
    column = lax.rem(lane, BOX)
    not_last = column < BOX - 1
    not_first = column > 0
    inner = jnp.where(low_half, jnp.where(row > 0, 1.0, 0.0), jnp.where(row < rows - 1, 1.0, 0.0))
    inside = []
    for k in range(planes + 2 * SWEEPS):
        x = first_plane + (k - SWEEPS)
        inside.append(jnp.where((x >= 0) & (x < n_orb * planes), 1.0, 0.0).astype(jnp.float32))

    def in_plane(field_in):
        swapped = pltpu.roll(field_in, BOX, 1)
        across = jnp.where(low_half, pltpu.roll(swapped, 1, 0), pltpu.roll(swapped, rows - 1, 0))
        upward = jnp.where(not_last, pltpu.roll(field_in, lanes - 1, 1), 0.0)
        downward = jnp.where(not_first, pltpu.roll(field_in, 1, 1), 0.0)
        return swapped + across * inner + upward + downward

    def contributions(p, pad, pad_back):
        first_at, second_at, offset_y, offset_z = refs[p, 0], refs[p, 1], refs[p, 2], refs[p, 3]
        first = slab[first_at].astype(jnp.float32)
        shifted = shift_cells(slab[second_at].astype(jnp.float32), offset_y, offset_z, pad)
        own = first * shifted
        density = []
        for ref, plane in before[0]:
            density.append(sides[ref][p, plane].astype(jnp.float32))
        density += [own[k] for k in range(planes)]
        for ref, plane in before[1]:
            density.append(sides[ref][p, plane].astype(jnp.float32))
        field = [coefficients[SWEEPS] * d for d in density]
        for sweep in range(SWEEPS):
            factor = coefficients[SWEEPS - 1 - sweep]
            low, high = sweep + 1, planes + 2 * SWEEPS - 1 - sweep
            after = [None] * len(field)
            for k in range(low, high):
                value = factor * density[k] + (field[k - 1] + field[k + 1] + in_plane(field[k]))
                if k < SWEEPS or k >= SWEEPS + planes:
                    value = value * inside[k]
                after[k] = value
            field = after
        potential = jnp.stack(field[SWEEPS:SWEEPS + planes])
        moved = shift_cells(potential * first, -offset_y, -offset_z, pad_back)
        return potential * shifted, moved

    def group(g, carry):
        pieces = []
        for u in range(width):
            pieces.append(contributions(g * width + u, pads.at[u], pads_back.at[u]))
        for u in range(width):
            p = g * width + u
            if last:
                forces[refs[p, 0]] += pieces[u][0]
                forces[refs[p, 1]] += pieces[u][1]
            else:
                given[p, 0] = pieces[u][0]
                given[p, 1] = pieces[u][1]
        return carry

    lax.fori_loop(0, refs.shape[0] // width, group, 0)

    if last:
        def finish(k, carry):
            rounded[k] = forces[k].astype(rounded.dtype)
            return carry

        lax.fori_loop(0, orbitals, finish, 0)


def reduce_parts(parts, n_orb, me):
    if n_orb & (n_orb - 1):
        return jnp.sum(
            lax.all_to_all(parts, "orb", split_axis=0, concat_axis=0, tiled=True), axis=0
        )
    bit = 1
    while bit < n_orb:
        upper = (me & bit) != 0
        halves = parts.reshape((-1, 2) + parts.shape[1:])
        low, high = halves[:, 0], halves[:, 1]
        sent = jnp.where(upper, low, high)
        kept = jnp.where(upper, high, low)
        parts = kept + lax.ppermute(sent, "orb", [(d, d ^ bit) for d in range(n_orb)])
        bit *= 2
    return parts


def slab_body(orbitals, pairs, tiles):
    n_orb = lax.axis_size("orb")
    orb_dev = orbitals.shape[0]
    order = chain(n_orb)
    position = [order.index(d) for d in range(n_orb)]
    exchange = functools.partial(
        lax.all_to_all, axis_name="orb", split_axis=0, concat_axis=0, tiled=True,
        axis_index_groups=[order],
    )
    seat = jnp.asarray(position, jnp.int32)
    me = lax.axis_index("orb")
    every = exchange(jnp.broadcast_to(pairs[None], (n_orb,) + pairs.shape)).reshape(-1, 4)

    ids = every[:, :2].reshape(-1)
    kinds = jnp.arange(n_orb * orb_dev, dtype=jnp.int32)
    named = jnp.any(ids[:, None] == kinds[None, :], axis=0).reshape(n_orb, orb_dev)
    locals_ = jnp.arange(orb_dev, dtype=jnp.int32)
    earlier = locals_[None, :] < locals_[:, None]
    before = jnp.sum((named[:, None, :] & earlier[None]).astype(jnp.int32), axis=2)
    total = jnp.sum(named.astype(jnp.int32), axis=1, keepdims=True)
    slots = jnp.where(named, before, total + locals_[None, :] - before)
    own_slots = lax.dynamic_index_in_dim(slots, me, 0, keepdims=False)
    chosen = jnp.sum(
        jnp.where(own_slots[None, :] == locals_[:, None], locals_[None, :], 0), axis=1
    ).astype(jnp.int32)

    def plan(capacity):
        return functools.partial(slab_plan, capacity, order, position, exchange)

    operands = (orbitals, every, tiles, slots, own_slots, chosen)
    capacity = orb_dev * 3 // 4
    return lax.cond(jnp.max(total) <= capacity, plan(capacity), plan(orb_dev), *operands)


def slab_plan(capacity, order, position, exchange, orbitals, every, tiles, slots, own_slots, chosen):
    n_orb = lax.axis_size("orb")
    orb_dev, box_planes, flat_cells = orbitals.shape
    planes = box_planes // n_orb
    rows = flat_cells // LANES
    seat = jnp.asarray(position, jnp.int32)
    me = lax.axis_index("orb")
    lines = pltpu.VMEM((box_planes * rows, LANES), jnp.float32)

    def leaving(first, count):
        return pl.pallas_call(
            spread_kernel,
            grid_spec=pltpu.PrefetchScalarGridSpec(
                num_scalar_prefetch=1,
                grid=(count,),
                in_specs=[
                    pl.BlockSpec((1, box_planes, flat_cells), lambda k, c: (c[first + k], 0, 0))
                ],
                out_specs=pl.BlockSpec(
                    (n_orb, 1, planes, rows, LANES), lambda k, c: (0, k, 0, 0, 0)
                ),
                scratch_shapes=[lines],
            ),
            out_shape=jax.ShapeDtypeStruct((n_orb, count, planes, rows, LANES), orbitals.dtype),
        )(chosen, orbitals)

    slab = exchange(leaving(0, capacity)).reshape(n_orb * capacity, planes, rows, LANES)
    ids = every[:, :2]
    owners = ids // orb_dev
    at = jnp.take(seat, owners) * capacity + jnp.take(slots.reshape(-1), ids)
    refs = jnp.concatenate([at, every[:, 2:]], axis=1)
    n_pairs = refs.shape[0]

    vmem = pl.BlockSpec(memory_space=pltpu.VMEM)
    smem = pl.BlockSpec(memory_space=pltpu.SMEM)
    limit = pltpu.CompilerParams(vmem_limit_bytes=58 * 1024 * 1024)
    fast = capacity < orb_dev
    chunks = 2 if fast and n_pairs % 8 == 0 else 1
    chunk = n_pairs // chunks
    group = math.gcd(chunk, 4) if fast else 1
    pair_group = math.gcd(chunk, 2) if fast else 1

    def pads(count):
        return pltpu.VMEM((count, planes, rows + 2 * PAD, LANES), jnp.float32)

    def density_of(chunk_refs):
        return pl.pallas_call(
            density_kernel,
            out_shape=jax.ShapeDtypeStruct((chunk, planes, rows, LANES), jnp.bfloat16),
            in_specs=[smem, vmem],
            out_specs=vmem,
            scratch_shapes=[pads(group)],
            compiler_params=limit,
            cost_estimate=pl.CostEstimate(
                flops=chunk * 400_000, bytes_accessed=12_000_000, transcendentals=0
            ),
        )(chunk_refs, slab)

    def halo_of(density):
        sides, lower, upper = [], [], []
        left = SWEEPS
        hop = 1
        while left > 0:
            width = min(planes, left)
            up = [(order[s], order[s + hop]) for s in range(n_orb - hop)]
            down = [(j, i) for i, j in up]
            sides.append(lax.ppermute(density[:, planes - width:], "orb", up))
            lower = [(len(sides) - 1, k) for k in range(width)] + lower
            sides.append(lax.ppermute(density[:, :width], "orb", down))
            upper = upper + [(len(sides) - 1, k) for k in range(width)]
            left -= width
            hop += 1
        return sides, (lower, upper)

    place = jnp.take(seat, me).reshape(1)
    chunk_refs = [refs[c * chunk:(c + 1) * chunk] for c in range(chunks)]
    halos = [halo_of(density_of(part)) for part in chunk_refs]

    field_shape = (n_orb * capacity, planes, rows, LANES)
    given = []
    for c in range(chunks - 1):
        sides, before = halos[c]
        given.append(pl.pallas_call(
            functools.partial(force_kernel, n_orb, before, polynomial(), False),
            out_shape=jax.ShapeDtypeStruct((chunk, 2, planes, rows, LANES), jnp.float32),
            in_specs=[smem, smem, vmem] + [vmem] * len(sides),
            out_specs=vmem,
            scratch_shapes=[pads(pair_group), pads(pair_group)],
            compiler_params=limit,
            cost_estimate=pl.CostEstimate(
                flops=chunk * 2_000_000, bytes_accessed=20_000_000, transcendentals=0
            ),
        )(chunk_refs[c], place, slab, *sides))
    sides, before = halos[-1]
    rest = None
    if fast:
        later = leaving(capacity, orb_dev - capacity)
        ready = given or sides
        rest = exchange(lax.optimization_barrier([later] + ready)[0])
        rest = rest.reshape(n_orb * (orb_dev - capacity), -1)
    if given:
        done_refs, done = refs[:(chunks - 1) * chunk], jnp.concatenate(given)
    else:
        done_refs, done = refs[:1], jnp.zeros((1, 2, planes, rows, LANES), jnp.float32)
    rounded = pl.pallas_call(
        functools.partial(force_kernel, n_orb, before, polynomial(), True),
        out_shape=jax.ShapeDtypeStruct(field_shape, jnp.bfloat16),
        in_specs=[smem, smem, vmem] + [vmem] * len(sides) + [smem, vmem],
        out_specs=vmem,
        scratch_shapes=[pltpu.VMEM(field_shape, jnp.float32), pads(pair_group), pads(pair_group)],
        compiler_params=limit,
        cost_estimate=pl.CostEstimate(
            flops=chunk * 3_000_000, bytes_accessed=30_000_000, transcendentals=0
        ),
    )(chunk_refs[-1], place, slab, *sides, done_refs, done)

    returned = exchange(rounded.reshape(n_orb, capacity, planes, rows, LANES))
    own_named = (own_slots < capacity).astype(jnp.int32)
    source = jnp.concatenate([jnp.minimum(own_slots, capacity - 1), own_named])
    exch_force = pl.pallas_call(
        collect_kernel,
        grid_spec=pltpu.PrefetchScalarGridSpec(
            num_scalar_prefetch=1,
            grid=(orb_dev,),
            in_specs=[
                pl.BlockSpec(
                    (n_orb, 1, planes, rows, LANES), lambda k, c: (0, c[k], 0, 0, 0)
                )
            ],
            out_specs=pl.BlockSpec((1, box_planes, flat_cells), lambda k, c: (k, 0, 0)),
            scratch_shapes=[lines],
        ),
        out_shape=jax.ShapeDtypeStruct((orb_dev, box_planes, flat_cells), jnp.float32),
        cost_estimate=pl.CostEstimate(
            flops=4_000_000, bytes_accessed=60_000_000, transcendentals=0
        ),
    )(source, returned)

    def against(left):
        return lax.dot_general(
            left, rounded.reshape(n_orb * capacity, -1), (((1,), (1,)), ((), ())),
            preferred_element_type=jnp.float32,
        ).reshape(n_orb, -1, n_orb, capacity)

    blocks = against(slab.reshape(n_orb * capacity, -1))
    ranks = jnp.arange(capacity, dtype=jnp.int32)
    own_part = jnp.sum(
        jnp.where(jnp.eye(n_orb, dtype=bool)[:, None, :, None]
                  & jnp.eye(capacity, dtype=bool)[None, :, None, :], blocks, 0.0), axis=(2, 3)
    )
    if rest is not None:
        blocks = jnp.concatenate([blocks, against(rest)], axis=1)
    blocks = blocks.transpose(0, 2, 1, 3).reshape(n_orb * n_orb, orb_dev * capacity)
    chosen_blocks = jnp.take(seat, tiles[:, 0]) * n_orb + jnp.take(seat, tiles[:, 1])
    picked = jnp.take(blocks, chosen_blocks, axis=0).reshape(-1, orb_dev, capacity)
    row_slots = jnp.take(slots, tiles[:, 0], axis=0)
    column_slots = jnp.take(slots, tiles[:, 1], axis=0)
    places = jnp.arange(orb_dev, dtype=jnp.int32)
    picked = jnp.sum(
        jnp.where((row_slots[:, :, None] == places)[..., None], picked[:, None], 0.0), axis=2
    )
    picked = jnp.sum(
        jnp.where((column_slots[:, :, None] == ranks)[:, None], picked[:, :, None, :], 0.0), axis=3
    )
    picked = picked.reshape(n_orb, -1)
    own_part = jnp.take(own_part, np.asarray(position), axis=0)
    self_part = jnp.sum(
        jnp.where(slots[:, :, None] == ranks, own_part[:, None, :], 0.0), axis=2
    )
    parts = jnp.concatenate([picked, self_part], axis=1)
    width = picked.shape[1]
    spare = -parts.shape[1] % (8 * LANES)
    parts = jnp.pad(parts, ((0, 0), (0, spare))).reshape(n_orb, -1, LANES)
    summed = reduce_parts(parts, n_orb, me).reshape(-1)
    tile_rows = summed[:width].reshape(-1, orb_dev * orb_dev)
    return exch_force, tile_rows * BOX ** (-1.5), summed[width:width + orb_dev] * BOX ** (-2.5)


def body(orbitals, pairs, tiles):
    planes, flat_cells = orbitals.shape[1:]
    n_orb = lax.axis_size("orb")
    if lax.axis_size("grid") == 1 and planes % n_orb == 0 and flat_cells % LANES == 0:
        return slab_body(orbitals, pairs, tiles)
    return general_body(orbitals, pairs, tiles)


def solution(mesh):
    in_specs = (P("orb", "grid", None), P("orb", None), P())
    out_specs = (P("orb", "grid", None), P(("grid", "orb"), None), P("orb"))
    return jax.shard_map(body, mesh=mesh, in_specs=in_specs, out_specs=out_specs, check_vma=False)
```

```python
import functools
import math

import jax
import jax.numpy as jnp
import numpy as np
from jax import lax
from jax.experimental import pallas as pl
from jax.experimental.pallas import tpu as pltpu
from jax.sharding import PartitionSpec as P

BOX = 64
SWEEPS = 3
SHIFT = 16
LANES = 128

SCREENING = 0.02
MIXING = 0.25


def padded_2(array, sides, width):
    for axis, dim in sides:
        devices, length = (lax.axis_size(axis), array.shape[dim])
        up = [(i, (i + 1) % devices) for i in range(devices - 1)]
        down = [(j, i) for i, j in up]
        last = lax.slice_in_dim(array, length - width, length, axis=dim)
        first = lax.slice_in_dim(array, 0, width, axis=dim)
        before = lax.ppermute(last, axis, up)
        after = lax.ppermute(first, axis, down)
        array = jnp.concatenate([before, array, after], axis=dim)
    return array


def operate_slab(field_in):
    padded = padded_2(field_in, (("grid", 1),), 1)
    beside = padded[:, 2:, :] + padded[:, :-2, :]
    zero_rows = jnp.zeros(field_in.shape[:-1] + (BOX,), jnp.float32)
    beside = beside + jnp.concatenate([field_in[..., BOX:], zero_rows], axis=-1)
    beside = beside + jnp.concatenate([zero_rows, field_in[..., :-BOX]], axis=-1)
    column = jnp.arange(BOX * BOX, dtype=jnp.int32) % BOX
    zero_cells = jnp.zeros(field_in.shape[:-1] + (1,), jnp.float32)
    upward = jnp.concatenate([field_in[..., 1:], zero_cells], axis=-1)
    downward = jnp.concatenate([zero_cells, field_in[..., :-1]], axis=-1)
    beside = (
        beside + jnp.where(column < BOX - 1, upward, 0.0) + jnp.where(column > 0, downward, 0.0)
    )
    return (6.0 + SCREENING) * field_in - beside


def chebyshev(density):
    center = 6.0 + SCREENING
    radius = 6.0
    ratio = center / radius
    residual = density
    direction = density / center
    solution = direction
    previous = 1.0 / ratio
    for sweep_index in range(SWEEPS):
        residual = residual - operate_slab(direction)
        current = 1.0 / (2.0 * ratio - previous)
        direction = current * previous * direction + 2.0 * current / radius * residual
        solution = solution + direction
        previous = current
    return solution


def move(field_in, offset_y, offset_z):
    cells = jnp.arange(BOX * BOX, dtype=jnp.int32)
    row_index = cells // BOX + offset_y
    col_index = cells % BOX + offset_z
    valid = (row_index >= 0) & (row_index < BOX) & (col_index >= 0) & (col_index < BOX)
    rolled = jnp.roll(field_in, -(offset_y * BOX + offset_z), axis=-1)
    return jnp.where(valid, rolled, 0.0)


def general_body(orbitals, pairs, tiles):
    n_orb = lax.axis_size("orb")
    orb_dev, planes, flat_cells = orbitals.shape
    pair_count = pairs.shape[0]
    ref_count = 2 * pair_count
    ref_orb = pairs[:, :2].reshape(ref_count)
    owner_index = ref_orb // orb_dev
    local_index = ref_orb % orb_dev
    capacity = (2 * pair_count + n_orb - 1) // n_orb + 1
    same_owner = owner_index[:, None] == owner_index[None, :]
    earlier = jnp.arange(ref_count)[None, :] < jnp.arange(ref_count)[:, None]
    slot_index = jnp.sum(same_owner & earlier, axis=1)
    target = owner_index * capacity + slot_index
    positions = jnp.arange(n_orb * capacity, dtype=jnp.int32)
    placed = target[None, :] == positions[:, None]
    request = jnp.max(jnp.where(placed, local_index[None, :], 0), axis=1).reshape(n_orb, capacity)
    asked = lax.all_to_all(request, "orb", split_axis=0, concat_axis=0, tiled=True)
    outgoing = jnp.take(orbitals, asked.reshape(-1), axis=0).reshape(
        n_orb, capacity, planes, flat_cells
    )
    incoming = lax.all_to_all(outgoing, "orb", split_axis=0, concat_axis=0, tiled=True)
    fetched = jnp.take(incoming.reshape(n_orb * capacity, planes, flat_cells), target, axis=0)
    fetched = fetched.reshape(pair_count, 2, planes, flat_cells)
    first_box = fetched[:, 0].astype(jnp.float32)
    second_box = fetched[:, 1].astype(jnp.float32)
    offset_y = pairs[:, 2]
    offset_z = pairs[:, 3]
    shifted = jax.vmap(move)(second_box, offset_y, offset_z)
    potential = chebyshev(first_box * shifted)
    to_first = -MIXING * potential * shifted
    to_second = -MIXING * jax.vmap(move)(potential * first_box, -offset_y, -offset_z)
    contrib = jnp.stack([to_first, to_second], axis=1).reshape(ref_count, planes * flat_cells)
    sending = jnp.dot(placed.astype(jnp.float32), contrib, precision=lax.Precision.HIGHEST)
    returned = lax.all_to_all(
        sending.reshape(n_orb, capacity, planes * flat_cells),
        "orb",
        split_axis=0,
        concat_axis=0,
        tiled=True,
    )
    owned = (asked.reshape(-1)[None, :] == jnp.arange(orb_dev, dtype=jnp.int32)[:, None]).astype(
        jnp.float32
    )
    exch_force = jnp.dot(
        owned,
        returned.reshape(n_orb * capacity, planes * flat_cells),
        precision=lax.Precision.HIGHEST,
    )
    rounded = exch_force.astype(jnp.bfloat16)
    own_rows = orbitals.reshape(orb_dev, planes * flat_cells)
    self_part = jnp.einsum("kc,kc->k", own_rows, rounded, preferred_element_type=jnp.float32)
    self_intersection = lax.psum(self_part, "grid") * BOX ** (-2.5)
    orbital_rows, force_rows = (
        lax.all_to_all(own_rows, "orb", split_axis=1, concat_axis=0, tiled=True),
        lax.all_to_all(rounded, "orb", split_axis=1, concat_axis=0, tiled=True),
    )
    intersection = lax.dot_general(
        orbital_rows, force_rows, (((1,), (1,)), ((), ())), preferred_element_type=jnp.float32
    )
    blocks = intersection.reshape(n_orb, orb_dev, n_orb, orb_dev).transpose(0, 2, 1, 3)
    blocks = blocks.reshape(n_orb * n_orb, orb_dev * orb_dev)
    picked = jnp.take(blocks, tiles[:, 0] * n_orb + tiles[:, 1], axis=0)
    summed = lax.psum_scatter(picked, ("grid", "orb"), scatter_dimension=0, tiled=True)
    return (
        exch_force.reshape(orb_dev, planes, flat_cells),
        summed * BOX ** (-1.5),
        self_intersection,
    )


def polynomial():
    center = 6.0 + SCREENING
    radius = 6.0
    ratio = center / radius
    residual = np.zeros(SWEEPS + 1)
    residual[0] = 1.0
    direction = residual / center
    total = direction.copy()
    previous = 1.0 / ratio
    for _ in range(SWEEPS):
        moved = np.concatenate([[0.0], direction[:-1]])
        residual = residual - (center * direction - moved)
        current = 1.0 / (2.0 * ratio - previous)
        direction = current * previous * direction + 2.0 * current / radius * residual
        total = total + direction
        previous = current
    return [-MIXING * float(value) for value in total]


def chain(n_orb):
    if n_orb % 8:
        return list(range(n_orb))
    order = []
    for layer in range(n_orb // 8):
        ring = [0, 1, 3, 2]
        for chip in ring if layer % 2 == 0 else ring[::-1]:
            order += [(layer * 4 + chip) * 2, (layer * 4 + chip) * 2 + 1]
    return order


PAD = 16


def shift_cells(field_in, offset_y, offset_z, pad):
    planes, rows, lanes = field_in.shape
    step = offset_y * BOX + offset_z
    down = lax.shift_right_arithmetic(step, jnp.int32(7))
    along = step - down * lanes
    turned = pltpu.roll(field_in.reshape(planes * rows, lanes), lax.rem(lanes - along, lanes), 1)
    pad[:, PAD:PAD + rows, :] = turned.reshape(planes, rows, lanes)
    near = pad[:, pl.ds(PAD + down, rows), :]
    far = pad[:, pl.ds(PAD + 1 + down, rows), :]
    lane = lax.broadcasted_iota(jnp.int32, (rows, lanes), 1)
    column = lax.rem(lane, BOX) + offset_z
    valid = (column >= 0) & (column < BOX)
    keep = valid & (lane < lanes - along)
    other = valid & (lane >= lanes - along)
    return jnp.where(keep[None], near, jnp.where(other[None], far, 0.0))


def density_kernel(refs, slab, out, pads):
    pads[...] = jnp.zeros_like(pads)
    width = pads.shape[0]

    def group(g, carry):
        values = []
        for u in range(width):
            p = g * width + u
            first = slab[refs[p, 0]].astype(jnp.float32)
            second = slab[refs[p, 1]].astype(jnp.float32)
            values.append(first * shift_cells(second, refs[p, 2], refs[p, 3], pads.at[u]))
        for u in range(width):
            out[g * width + u] = values[u].astype(out.dtype)
        return carry

    lax.fori_loop(0, out.shape[0] // width, group, 0)


def spread_kernel(chosen, own, out, lines):
    box_planes, flat_cells = own.shape[1:]
    slabs, _, planes, rows, lanes = out.shape
    for r in range(rows):
        lines[pl.ds(r, box_planes, stride=rows), :] = own[0, :, r * lanes:(r + 1) * lanes].astype(
            jnp.float32
        )
    out[...] = lines[...].reshape(out.shape).astype(out.dtype)


def orb_count(slots):
    return slots.shape[0] // 2


def collect_kernel(slots, back, out, lines):
    box_planes, flat_cells = out.shape[1:]
    slabs, _, planes, rows, lanes = back.shape
    named = slots[orb_count(slots) + pl.program_id(0)] > 0
    values = back[...].astype(jnp.float32).reshape(lines.shape)
    lines[...] = jnp.where(named, values, 0.0)
    for r in range(rows):
        out[0, :, r * lanes:(r + 1) * lanes] = lines[pl.ds(r, box_planes, stride=rows), :]


def force_kernel(n_orb, before, coefficients, last, refs, place, slab, *rest):
    if last:
        sides = rest[:-6]
        all_refs, earlier, rounded, forces, pads, pads_back = rest[-6:]
    else:
        sides = rest[:-3]
        given, pads, pads_back = rest[-3:]
    orbitals, planes, rows, lanes = slab.shape
    width = pads.shape[0]
    pads[...] = jnp.zeros_like(pads)
    pads_back[...] = jnp.zeros_like(pads_back)

    if last:
        def clear(k, carry):
            forces[k] = jnp.zeros(forces.shape[1:], jnp.float32)
            return carry

        lax.fori_loop(0, orbitals, clear, 0)

        def add(p, carry):
            forces[all_refs[p, 0]] += earlier[p, 0]
            forces[all_refs[p, 1]] += earlier[p, 1]
            return carry

        lax.fori_loop(0, earlier.shape[0], add, 0)

    first_plane = place[0] * planes
    lane = lax.broadcasted_iota(jnp.int32, (rows, lanes), 1)
    row = lax.broadcasted_iota(jnp.int32, (rows, lanes), 0)
    low_half = lane < BOX
    column = lax.rem(lane, BOX)
    not_last = column < BOX - 1
    not_first = column > 0
    inner = jnp.where(low_half, jnp.where(row > 0, 1.0, 0.0), jnp.where(row < rows - 1, 1.0, 0.0))
    inside = []
    for k in range(planes + 2 * SWEEPS):
        x = first_plane + (k - SWEEPS)
        inside.append(jnp.where((x >= 0) & (x < n_orb * planes), 1.0, 0.0).astype(jnp.float32))

    def in_plane(field_in):
        swapped = pltpu.roll(field_in, BOX, 1)
        across = jnp.where(low_half, pltpu.roll(swapped, 1, 0), pltpu.roll(swapped, rows - 1, 0))
        upward = jnp.where(not_last, pltpu.roll(field_in, lanes - 1, 1), 0.0)
        downward = jnp.where(not_first, pltpu.roll(field_in, 1, 1), 0.0)
        return swapped + across * inner + upward + downward

    def contributions(p, pad, pad_back):
        first_at, second_at, offset_y, offset_z = refs[p, 0], refs[p, 1], refs[p, 2], refs[p, 3]
        first = slab[first_at].astype(jnp.float32)
        shifted = shift_cells(slab[second_at].astype(jnp.float32), offset_y, offset_z, pad)
        own = first * shifted
        density = []
        for ref, plane in before[0]:
            density.append(sides[ref][p, plane].astype(jnp.float32))
        density += [own[k] for k in range(planes)]
        for ref, plane in before[1]:
            density.append(sides[ref][p, plane].astype(jnp.float32))
        field = [coefficients[SWEEPS] * d for d in density]
        for sweep in range(SWEEPS):
            factor = coefficients[SWEEPS - 1 - sweep]
            low, high = sweep + 1, planes + 2 * SWEEPS - 1 - sweep
            after = [None] * len(field)
            for k in range(low, high):
                value = factor * density[k] + (field[k - 1] + field[k + 1] + in_plane(field[k]))
                if k < SWEEPS or k >= SWEEPS + planes:
                    value = value * inside[k]
                after[k] = value
            field = after
        potential = jnp.stack(field[SWEEPS:SWEEPS + planes])
        moved = shift_cells(potential * first, -offset_y, -offset_z, pad_back)
        return potential * shifted, moved

    def group(g, carry):
        pieces = []
        for u in range(width):
            pieces.append(contributions(g * width + u, pads.at[u], pads_back.at[u]))
        for u in range(width):
            p = g * width + u
            if last:
                forces[refs[p, 0]] += pieces[u][0]
                forces[refs[p, 1]] += pieces[u][1]
            else:
                given[p, 0] = pieces[u][0]
                given[p, 1] = pieces[u][1]
        return carry

    lax.fori_loop(0, refs.shape[0] // width, group, 0)

    if last:
        def finish(k, carry):
            rounded[k] = forces[k].astype(rounded.dtype)
            return carry

        lax.fori_loop(0, orbitals, finish, 0)


def reduce_parts(parts, n_orb, me):
    if n_orb & (n_orb - 1):
        return jnp.sum(
            lax.all_to_all(parts, "orb", split_axis=0, concat_axis=0, tiled=True), axis=0
        )
    bit = 1
    while bit < n_orb:
        upper = (me & bit) != 0
        halves = parts.reshape((-1, 2) + parts.shape[1:])
        low, high = halves[:, 0], halves[:, 1]
        sent = jnp.where(upper, low, high)
        kept = jnp.where(upper, high, low)
        parts = kept + lax.ppermute(sent, "orb", [(d, d ^ bit) for d in range(n_orb)])
        bit *= 2
    return parts


def slab_body(orbitals, pairs, tiles):
    n_orb = lax.axis_size("orb")
    orb_dev = orbitals.shape[0]
    order = chain(n_orb)
    position = [order.index(d) for d in range(n_orb)]
    exchange = functools.partial(
        lax.all_to_all, axis_name="orb", split_axis=0, concat_axis=0, tiled=True,
        axis_index_groups=[order],
    )
    seat = jnp.asarray(position, jnp.int32)
    me = lax.axis_index("orb")
    every = exchange(jnp.broadcast_to(pairs[None], (n_orb,) + pairs.shape)).reshape(-1, 4)

    ids = every[:, :2].reshape(-1)
    kinds = jnp.arange(n_orb * orb_dev, dtype=jnp.int32)
    named = jnp.any(ids[:, None] == kinds[None, :], axis=0).reshape(n_orb, orb_dev)
    locals_ = jnp.arange(orb_dev, dtype=jnp.int32)
    earlier = locals_[None, :] < locals_[:, None]
    before = jnp.sum((named[:, None, :] & earlier[None]).astype(jnp.int32), axis=2)
    total = jnp.sum(named.astype(jnp.int32), axis=1, keepdims=True)
    slots = jnp.where(named, before, total + locals_[None, :] - before)
    own_slots = lax.dynamic_index_in_dim(slots, me, 0, keepdims=False)
    chosen = jnp.sum(
        jnp.where(own_slots[None, :] == locals_[:, None], locals_[None, :], 0), axis=1
    ).astype(jnp.int32)

    def plan(capacity):
        return functools.partial(slab_plan, capacity, order, position, exchange)

    operands = (orbitals, every, tiles, slots, own_slots, chosen)
    capacity = orb_dev * 3 // 4
    return lax.cond(jnp.max(total) <= capacity, plan(capacity), plan(orb_dev), *operands)


def slab_plan(capacity, order, position, exchange, orbitals, every, tiles, slots, own_slots, chosen):
    n_orb = lax.axis_size("orb")
    orb_dev, box_planes, flat_cells = orbitals.shape
    planes = box_planes // n_orb
    rows = flat_cells // LANES
    seat = jnp.asarray(position, jnp.int32)
    me = lax.axis_index("orb")
    lines = pltpu.VMEM((box_planes * rows, LANES), jnp.float32)

    def leaving(first, count):
        return pl.pallas_call(
            spread_kernel,
            grid_spec=pltpu.PrefetchScalarGridSpec(
                num_scalar_prefetch=1,
                grid=(count,),
                in_specs=[
                    pl.BlockSpec((1, box_planes, flat_cells), lambda k, c: (c[first + k], 0, 0))
                ],
                out_specs=pl.BlockSpec(
                    (n_orb, 1, planes, rows, LANES), lambda k, c: (0, k, 0, 0, 0)
                ),
                scratch_shapes=[lines],
            ),
            out_shape=jax.ShapeDtypeStruct((n_orb, count, planes, rows, LANES), orbitals.dtype),
        )(chosen, orbitals)

    slab = exchange(leaving(0, capacity)).reshape(n_orb * capacity, planes, rows, LANES)
    ids = every[:, :2]
    owners = ids // orb_dev
    at = jnp.take(seat, owners) * capacity + jnp.take(slots.reshape(-1), ids)
    refs = jnp.concatenate([at, every[:, 2:]], axis=1)
    n_pairs = refs.shape[0]

    vmem = pl.BlockSpec(memory_space=pltpu.VMEM)
    smem = pl.BlockSpec(memory_space=pltpu.SMEM)
    limit = pltpu.CompilerParams(vmem_limit_bytes=58 * 1024 * 1024)
    fast = capacity < orb_dev
    chunks = 2 if fast and n_pairs % 8 == 0 else 1
    chunk = n_pairs // chunks
    group = math.gcd(chunk, 4) if fast else 1
    pair_group = math.gcd(chunk, 2) if fast else 1

    def pads(count):
        return pltpu.VMEM((count, planes, rows + 2 * PAD, LANES), jnp.float32)

    def density_of(chunk_refs):
        return pl.pallas_call(
            density_kernel,
            out_shape=jax.ShapeDtypeStruct((chunk, planes, rows, LANES), jnp.bfloat16),
            in_specs=[smem, vmem],
            out_specs=vmem,
            scratch_shapes=[pads(group)],
            compiler_params=limit,
            cost_estimate=pl.CostEstimate(
                flops=chunk * 400_000, bytes_accessed=12_000_000, transcendentals=0
            ),
        )(chunk_refs, slab)

    def halo_of(density):
        sides, lower, upper = [], [], []
        left = SWEEPS
        hop = 1
        while left > 0:
            width = min(planes, left)
            up = [(order[s], order[s + hop]) for s in range(n_orb - hop)]
            down = [(j, i) for i, j in up]
            sides.append(lax.ppermute(density[:, planes - width:], "orb", up))
            lower = [(len(sides) - 1, k) for k in range(width)] + lower
            sides.append(lax.ppermute(density[:, :width], "orb", down))
            upper = upper + [(len(sides) - 1, k) for k in range(width)]
            left -= width
            hop += 1
        return sides, (lower, upper)

    place = jnp.take(seat, me).reshape(1)
    chunk_refs = [refs[c * chunk:(c + 1) * chunk] for c in range(chunks)]
    densities = [density_of(part) for part in chunk_refs]
    halos = [halo_of(density) for density in densities]
    if chunks > 1:
        chunk_refs[0] = lax.optimization_barrier((chunk_refs[0], densities[-1]))[0]

    field_shape = (n_orb * capacity, planes, rows, LANES)
    given = []
    for c in range(chunks - 1):
        sides, before = halos[c]
        given.append(pl.pallas_call(
            functools.partial(force_kernel, n_orb, before, polynomial(), False),
            out_shape=jax.ShapeDtypeStruct((chunk, 2, planes, rows, LANES), jnp.float32),
            in_specs=[smem, smem, vmem] + [vmem] * len(sides),
            out_specs=vmem,
            scratch_shapes=[pads(pair_group), pads(pair_group)],
            compiler_params=limit,
            cost_estimate=pl.CostEstimate(
                flops=chunk * 2_000_000, bytes_accessed=20_000_000, transcendentals=0
            ),
        )(chunk_refs[c], place, slab, *sides))
    sides, before = halos[-1]
    rest = None
    if fast:
        later = leaving(capacity, orb_dev - capacity)
        ready = given + sides
        rest = exchange(lax.optimization_barrier([later] + ready)[0])
        rest = rest.reshape(n_orb * (orb_dev - capacity), -1)
    if given:
        done_refs, done = refs[:(chunks - 1) * chunk], jnp.concatenate(given)
    else:
        done_refs, done = refs[:1], jnp.zeros((1, 2, planes, rows, LANES), jnp.float32)
    rounded = pl.pallas_call(
        functools.partial(force_kernel, n_orb, before, polynomial(), True),
        out_shape=jax.ShapeDtypeStruct(field_shape, jnp.bfloat16),
        in_specs=[smem, smem, vmem] + [vmem] * len(sides) + [smem, vmem],
        out_specs=vmem,
        scratch_shapes=[pltpu.VMEM(field_shape, jnp.float32), pads(pair_group), pads(pair_group)],
        compiler_params=limit,
        cost_estimate=pl.CostEstimate(
            flops=chunk * 3_000_000, bytes_accessed=30_000_000, transcendentals=0
        ),
    )(chunk_refs[-1], place, slab, *sides, done_refs, done)

    returned = exchange(rounded.reshape(n_orb, capacity, planes, rows, LANES))
    own_named = (own_slots < capacity).astype(jnp.int32)
    source = jnp.concatenate([jnp.minimum(own_slots, capacity - 1), own_named])
    exch_force = pl.pallas_call(
        collect_kernel,
        grid_spec=pltpu.PrefetchScalarGridSpec(
            num_scalar_prefetch=1,
            grid=(orb_dev,),
            in_specs=[
                pl.BlockSpec(
                    (n_orb, 1, planes, rows, LANES), lambda k, c: (0, c[k], 0, 0, 0)
                )
            ],
            out_specs=pl.BlockSpec((1, box_planes, flat_cells), lambda k, c: (k, 0, 0)),
            scratch_shapes=[lines],
        ),
        out_shape=jax.ShapeDtypeStruct((orb_dev, box_planes, flat_cells), jnp.float32),
        cost_estimate=pl.CostEstimate(
            flops=4_000_000, bytes_accessed=60_000_000, transcendentals=0
        ),
    )(source, returned)

    def against(left):
        return lax.dot_general(
            left, rounded.reshape(n_orb * capacity, -1), (((1,), (1,)), ((), ())),
            preferred_element_type=jnp.float32,
        ).reshape(n_orb, -1, n_orb, capacity)

    blocks = against(slab.reshape(n_orb * capacity, -1))
    ranks = jnp.arange(capacity, dtype=jnp.int32)
    own_part = jnp.sum(
        jnp.where(jnp.eye(n_orb, dtype=bool)[:, None, :, None]
                  & jnp.eye(capacity, dtype=bool)[None, :, None, :], blocks, 0.0), axis=(2, 3)
    )
    if rest is not None:
        blocks = jnp.concatenate([blocks, against(rest)], axis=1)
    blocks = blocks.transpose(0, 2, 1, 3).reshape(n_orb * n_orb, orb_dev * capacity)
    chosen_blocks = jnp.take(seat, tiles[:, 0]) * n_orb + jnp.take(seat, tiles[:, 1])
    picked = jnp.take(blocks, chosen_blocks, axis=0).reshape(-1, orb_dev, capacity)
    row_slots = jnp.take(slots, tiles[:, 0], axis=0)
    column_slots = jnp.take(slots, tiles[:, 1], axis=0)
    places = jnp.arange(orb_dev, dtype=jnp.int32)
    picked = jnp.sum(
        jnp.where((row_slots[:, :, None] == places)[..., None], picked[:, None], 0.0), axis=2
    )
    picked = jnp.sum(
        jnp.where((column_slots[:, :, None] == ranks)[:, None], picked[:, :, None, :], 0.0), axis=3
    )
    picked = picked.reshape(n_orb, -1)
    own_part = jnp.take(own_part, np.asarray(position), axis=0)
    self_part = jnp.sum(
        jnp.where(slots[:, :, None] == ranks, own_part[:, None, :], 0.0), axis=2
    )
    parts = jnp.concatenate([picked, self_part], axis=1)
    width = picked.shape[1]
    spare = -parts.shape[1] % (8 * LANES)
    parts = jnp.pad(parts, ((0, 0), (0, spare))).reshape(n_orb, -1, LANES)
    summed = reduce_parts(parts, n_orb, me).reshape(-1)
    tile_rows = summed[:width].reshape(-1, orb_dev * orb_dev)
    return exch_force, tile_rows * BOX ** (-1.5), summed[width:width + orb_dev] * BOX ** (-2.5)


def body(orbitals, pairs, tiles):
    planes, flat_cells = orbitals.shape[1:]
    n_orb = lax.axis_size("orb")
    if lax.axis_size("grid") == 1 and planes % n_orb == 0 and flat_cells % LANES == 0:
        return slab_body(orbitals, pairs, tiles)
    return general_body(orbitals, pairs, tiles)


def solution(mesh):
    in_specs = (P("orb", "grid", None), P("orb", None), P())
    out_specs = (P("orb", "grid", None), P(("grid", "orb"), None), P("orb"))
    return jax.shard_map(body, mesh=mesh, in_specs=in_specs, out_specs=out_specs, check_vma=False)
```
